128 devices in a mesh: ctx: 16 (over z, y), lag: 4 (over x_lo, core), chan: 2 (over x_hi).
Axes of the slice: x: 4 (x_hi: 2, x_lo: 2; x = x_hi * 2 + x_lo), y: 4, z: 4, core: 2. Of those that a mesh axis runs over, the one named last changes fastest.
Arguments:
- values: bfloat16 [2048, 8192], P('ctx', 'chan'), may hold values from -6 to 6
- gate: bfloat16 [2048, 8192], P('ctx', ('chan', 'lag')), may hold values from -6 to 6
- bias: float32 [8192], P('chan'), may hold values from -6 to 6
- filter_taps: bfloat16 [2048, 8192], P('ctx', 'chan'), may hold values from -2 to 2
Outputs:
- mixed: bfloat16 [2048, 8192], P('ctx', ('chan', 'lag'))
The draws below stay inside these ranges and needn't reach their ends.
All inputs are finite; a program needn't handle non-finite values.
Results may differ from the reference program's by a relative error of at most 0.006.
Values may be sent and summed in bfloat16 or wider, within the bound.
A program may use at most 64 MiB of HBM per device.

```python
import math
import jax
import jax.numpy as jnp

CHANNELS = 8192
STREAM_ITEMS = 2048


def draw_filter_taps(key, part):
    stochastic_seeds = jax.random.split(jax.random.fold_in(key, 7), 6)
    item_step_index = jnp.arange(STREAM_ITEMS, dtype=jnp.float32)[:, None]
    share_slow = 0.5
    slow = jax.random.uniform(stochastic_seeds[0], (1, CHANNELS)) < share_slow
    slow_rate = jnp.exp(jax.random.uniform(stochastic_seeds[1], (1, CHANNELS), minval=math.log(0.05), maxval=math.log(0.6))) / STREAM_ITEMS
    fast_rate = jnp.exp(jax.random.uniform(stochastic_seeds[2], (1, CHANNELS), minval=math.log(1.0 / 50.0), maxval=math.log(1.0 / 30.0)))
    rates = jnp.where(slow, slow_rate, fast_rate)
    spike_onset_step = jax.random.randint(stochastic_seeds[3], (2,), 1, STREAM_ITEMS).astype(jnp.float32)
    falloff_factors = jax.random.uniform(stochastic_seeds[4], (2, CHANNELS), minval=0.2, maxval=0.5)
    logarithmic_amplitude_profile = -rates * item_step_index
    logarithmic_amplitude_profile = logarithmic_amplitude_profile + jnp.where(item_step_index >= spike_onset_step[0], jnp.log(1.0 - falloff_factors[0])[None, :], 0.0)
    logarithmic_amplitude_profile = logarithmic_amplitude_profile + jnp.where(item_step_index >= spike_onset_step[1], jnp.log(1.0 - falloff_factors[1])[None, :], 0.0)
    envelope = jnp.exp(logarithmic_amplitude_profile)
    noise = jnp.clip(jax.random.normal(stochastic_seeds[5], (STREAM_ITEMS, CHANNELS), jnp.float32), -5.0, 5.0)
    scale = 1.0 / jnp.sqrt(jnp.sum(envelope * envelope, axis=0, keepdims=True))
    return jnp.clip(noise * envelope * scale, -2.0, 2.0).astype(jnp.bfloat16)


def shard_levels(key, dims, cuts, smallest, high):
    factor_of, own = 1.0, jax.random.fold_in(key, 6)
    for dim, parts in cuts:
        steps = jnp.exp(jax.random.uniform(jax.random.fold_in(own, dim), (parts,), jnp.float32, smallest / len(cuts), high / len(cuts)))
        factor_of = factor_of * jnp.repeat(steps, dims[dim] // parts).reshape([-1 if axis == dim else 1 for axis in range(len(dims))])
    return factor_of


def gaussian(key, shape, width, limit, shards=(), kind=jnp.bfloat16):
    drawn = width * jax.random.normal(key, shape, jnp.float32)
    if shards:
        drawn = drawn * shard_levels(key, shape, shards, -0.22, 0.18)
    return jnp.clip(drawn, -limit, limit).astype(kind)


def setup_inputs(seed: int = 0) -> dict:
    key_list = jax.random.split(jax.random.key(seed), 5)
    return {
        "values": gaussian(key_list[0], (STREAM_ITEMS, CHANNELS), 1.0, 6.0, ((0, 16), (1, 2))),
        "gate": gaussian(key_list[1], (STREAM_ITEMS, CHANNELS), 1.0, 6.0, ((0, 16), (1, 8))),
        "bias": gaussian(key_list[2], (CHANNELS,), 1.0, 6.0, ((0, 2),), jnp.float32),
        "filter_taps": draw_filter_taps(jax.random.fold_in(key_list[4], 71), 0),
    }


def reference(values, gate, bias, filter_taps):
    value_data = values.astype(jnp.float32)
    taps_data = filter_taps.astype(jnp.float32)
    padded_length = 2 * STREAM_ITEMS
    value_freq = jnp.fft.rfft(value_data, n=padded_length, axis=0)
    taps_freq = jnp.fft.rfft(taps_data, n=padded_length, axis=0)
    convolved = jnp.fft.irfft(value_freq * taps_freq, n=padded_length, axis=0)[:STREAM_ITEMS]
    convolved = convolved.astype(jnp.float32)
    mixed = gate.astype(jnp.float32) * (convolved + bias[None, :] * value_data)
    return mixed.astype(jnp.bfloat16)
```

```python
import functools
import math

import jax
import jax.numpy as jnp
import numpy as np
from jax import lax
from jax.experimental import pallas as pl
from jax.experimental.pallas import tpu as pltpu
from jax.sharding import PartitionSpec as P

MESH = pl.DeviceIdType.MESH
LANES = 128
HALF = 64
SIDE = 4


def halves(table):
    upper = table.astype(jnp.bfloat16)
    lower = (table - upper.astype(np.float64)).astype(jnp.bfloat16)
    return upper, lower


def tables(rows):
    length = 2 * rows
    order = np.arange(rows)
    freq = np.where(order < rows // 2, 2 * order, 2 * (order - rows // 2) + 1)
    token = np.arange(rows)
    angle = 2.0 * math.pi * ((freq[:, None] * token[None, :]) % length) / length
    alternate = np.where(token % 2 == 0, 1.0, -1.0)
    real, imag = np.cos(angle), -np.sin(angle)
    imag[0] = alternate
    weight = np.where(order == 0, 1.0, 2.0) / length
    back_real = (real * weight[:, None]).T
    back_imag = (imag * weight[:, None]).T
    back_imag[:, 0] = -alternate / length
    forward = np.concatenate([real, imag], axis=0)
    backward = np.concatenate([back_real, back_imag], axis=1)
    return halves(forward), halves(backward)


def hops(offset):
    return sum(min(part, SIDE - part) for part in divmod(offset, SIDE))


def peer_of(me, offset, count):
    dz, dy = divmod(offset, SIDE)
    z, y = me // SIDE, me % SIDE
    return ((z + dz) % (count // SIDE)) * SIDE + (y + dy) % SIDE


def kernel(
    count,
    values_hbm,
    taps_hbm,
    gate_hbm,
    bias_hbm,
    fwd_hi_hbm,
    fwd_lo_hbm,
    inv_hi_hbm,
    inv_lo_hbm,
    out_ref,
    vbuf,
    tbuf,
    gbuf,
    bbuf,
    fwd_hi,
    fwd_lo,
    inv_hi,
    inv_lo,
    packed,
    blocks,
    spec_a,
    sum_a,
    spec_b,
    sum_b,
    total,
    ret_send,
    ret_recv,
    load_sem,
    send_sem,
    recv_sem,
    back_send_sem,
    back_recv_sem,
):
    me = lax.axis_index("ctx")
    lag = lax.axis_index("lag")
    rows = vbuf.shape[0]
    share = vbuf.shape[1]
    tiles = share // LANES
    offsets = sorted(range(1, count), key=lambda o: -hops(o))

    barrier = pltpu.get_barrier_semaphore()
    for offset in offsets:
        pl.semaphore_signal(
            barrier, inc=1, device_id={"ctx": peer_of(me, offset, count)}, device_id_type=MESH
        )

    columns = pl.ds(pl.multiple_of(lag * share, share), share)
    loads = [
        pltpu.make_async_copy(src, dst, load_sem.at[i])
        for i, (src, dst) in enumerate(
            [
                (taps_hbm.at[:, columns], tbuf),
                (values_hbm.at[:, columns], vbuf),
                (fwd_hi_hbm, fwd_hi),
                (fwd_lo_hbm, fwd_lo),
                (inv_hi_hbm, inv_hi),
                (inv_lo_hbm, inv_lo),
                (bias_hbm.at[:, columns], bbuf),
                (gate_hbm, gbuf),
            ]
        )
    ]
    for load in loads:
        load.start()
    loads[0].wait()
    loads[1].wait()

    lower = lax.broadcasted_iota(jnp.int32, (rows, LANES), 1) < HALF
    for tile in range(tiles):
        lanes = slice(tile * LANES, (tile + 1) * LANES)
        value = vbuf[:, lanes].astype(jnp.float32)
        tap = pltpu.roll(tbuf[:, lanes].astype(jnp.float32), HALF, 1)
        packed[2 * tile] = jnp.where(lower, value, tap).astype(jnp.bfloat16)
        packed[2 * tile + 1] = jnp.where(lower, tap, value).astype(jnp.bfloat16)
    blocks[me] = packed[me]

    pl.semaphore_wait(barrier, count - 1)
    sends = []
    for i, offset in enumerate(offsets):
        peer = peer_of(me, offset, count)
        copy = pltpu.make_async_remote_copy(
            src_ref=packed.at[peer],
            dst_ref=blocks.at[me],
            send_sem=send_sem.at[i],
            recv_sem=recv_sem.at[me],
            device_id={"ctx": peer},
            device_id_type=MESH,
        )
        copy.start()
        sends.append(copy)
    for load in loads[2:]:
        load.wait()

    def transform(block):
        data = blocks[block]
        spectrum = jnp.dot(fwd_hi[...], data, preferred_element_type=jnp.float32)
        spectrum = spectrum + jnp.dot(fwd_lo[...], data, preferred_element_type=jnp.float32)
        turned = pltpu.roll(spectrum, HALF, 1)
        spec_a[block] = spectrum
        spec_b[block] = turned
        sum_a[block] = spectrum[:rows] + spectrum[rows:]
        sum_b[block] = turned[:rows] + turned[rows:]

    transform(me)
    for offset in reversed(offsets):
        source = peer_of(me, offset, count)
        pltpu.make_async_remote_copy(
            src_ref=packed.at[source],
            dst_ref=blocks.at[source],
            send_sem=send_sem.at[0],
            recv_sem=recv_sem.at[source],
            device_id={"ctx": source},
            device_id_type=MESH,
        ).wait_recv()
        transform(source)

    group_rows = 8
    sub = lax.broadcasted_iota(jnp.int32, (group_rows, LANES), 0)

    def group(step, carry):
        start = pl.multiple_of(step * group_rows, group_rows)
        real_rows = pl.ds(start, group_rows)
        imag_rows = pl.ds(pl.multiple_of(rows + start, group_rows), group_rows)
        mask = jnp.where(sub + start > 0, 1.0, 0.0)
        sign = jnp.where(step < rows // group_rows // 2, 1.0, -1.0)
        acc = [None] * count
        for a in range(count // 2):
            left = (spec_a[a, real_rows], spec_a[a, imag_rows], sum_a[a, real_rows])
            for b in range(a, count - a):
                right = (spec_b[b, real_rows], spec_b[b, imag_rows], sum_b[b, real_rows])
                if a == b:
                    right = tuple(0.5 * r for r in right)
                terms = tuple(x * y for x, y in zip(left, right))
                old = acc[a + b]
                acc[a + b] = terms if old is None else tuple(x + y for x, y in zip(old, terms))
        before = None
        for n in range(count):
            first, second, third = acc[n]
            now = (first - mask * second, mask * (third - first) - second)
            if before is None:
                mixed = now
            else:
                mixed = (now[0] + sign * before[0], now[1] + sign * before[1])
            total[n, real_rows] = mixed[0]
            total[n, imag_rows] = mixed[1]
            before = now
        return carry

    lax.fori_loop(0, rows // group_rows, group, 0)

    lower_half = lax.broadcasted_iota(jnp.int32, (rows // 2, LANES), 1) < HALF

    def restore(block):
        spectrum = total[block].astype(jnp.bfloat16)
        result = jnp.dot(inv_hi[...], spectrum, preferred_element_type=jnp.float32)
        result = result + jnp.dot(inv_lo[...], spectrum, preferred_element_type=jnp.float32)
        top, bottom = result[: rows // 2], result[rows // 2 :]
        kept = jnp.where(lower_half, top, bottom)
        moved = pltpu.roll(jnp.where(lower_half, bottom, top), HALF, 1)
        return (kept + moved).astype(jnp.bfloat16)

    backs = []
    for i, offset in enumerate(offsets):
        peer = peer_of(me, offset, count)
        ret_send[peer] = restore(peer)
        copy = pltpu.make_async_remote_copy(
            src_ref=ret_send.at[peer],
            dst_ref=ret_recv.at[me],
            send_sem=back_send_sem.at[i],
            recv_sem=back_recv_sem.at[me],
            device_id={"ctx": peer},
            device_id_type=MESH,
        )
        copy.start()
        backs.append(copy)
    ret_recv[me] = restore(me)
    for copy in sends:
        copy.wait_send()
    for offset in reversed(offsets):
        source = peer_of(me, offset, count)
        pltpu.make_async_remote_copy(
            src_ref=ret_send.at[source],
            dst_ref=ret_recv.at[source],
            send_sem=back_send_sem.at[0],
            recv_sem=back_recv_sem.at[source],
            device_id={"ctx": source},
            device_id_type=MESH,
        ).wait_recv()
    for tile in range(tiles):
        lanes = slice(tile * LANES, (tile + 1) * LANES)
        even = ret_recv[2 * tile].astype(jnp.float32)
        odd = ret_recv[2 * tile + 1].astype(jnp.float32)
        top = jnp.where(lower_half, even, pltpu.roll(odd, HALF, 1))
        bottom = jnp.where(lower_half, pltpu.roll(even, HALF, 1), odd)
        skip = bbuf[:, lanes]
        for part, conv in ((slice(0, rows // 2), top), (slice(rows // 2, rows), bottom)):
            value = vbuf[part, lanes].astype(jnp.float32)
            gate = gbuf[part, lanes].astype(jnp.float32)
            out_ref[part, lanes] = (gate * (conv + skip * value)).astype(jnp.bfloat16)
    for copy in backs:
        copy.wait_send()


def solution(mesh):
    count = mesh.shape["ctx"]
    lag_count = mesh.shape["lag"]

    def body(values, gate, bias, filter_taps):
        rows = values.shape[0]
        share = values.shape[1] // lag_count
        (fwd_hi, fwd_lo), (inv_hi, inv_lo) = tables(rows)
        any_spec = pl.BlockSpec(memory_space=pl.ANY)
        bf16, f32 = jnp.bfloat16, jnp.float32
        return pl.pallas_call(
            functools.partial(kernel, count),
            out_shape=jax.ShapeDtypeStruct((rows, share), bf16),
            in_specs=[any_spec] * 8,
            out_specs=pl.BlockSpec(memory_space=pltpu.VMEM),
            scratch_shapes=[
                pltpu.VMEM((rows, share), bf16),
                pltpu.VMEM((rows, share), bf16),
                pltpu.VMEM((rows, share), bf16),
                pltpu.VMEM((1, share), f32),
                pltpu.VMEM((2 * rows, rows), bf16),
                pltpu.VMEM((2 * rows, rows), bf16),
                pltpu.VMEM((rows, 2 * rows), bf16),
                pltpu.VMEM((rows, 2 * rows), bf16),
                pltpu.VMEM((count, rows, LANES), bf16),
                pltpu.VMEM((count, rows, LANES), bf16),
                pltpu.VMEM((count, 2 * rows, LANES), f32),
                pltpu.VMEM((count, rows, LANES), f32),
                pltpu.VMEM((count, 2 * rows, LANES), f32),
                pltpu.VMEM((count, rows, LANES), f32),
                pltpu.VMEM((count, 2 * rows, LANES), f32),
                pltpu.VMEM((count, rows // 2, LANES), bf16),
                pltpu.VMEM((count, rows // 2, LANES), bf16),
                pltpu.SemaphoreType.DMA((8,)),
                pltpu.SemaphoreType.DMA((count,)),
                pltpu.SemaphoreType.DMA((count,)),
                pltpu.SemaphoreType.DMA((count,)),
                pltpu.SemaphoreType.DMA((count,)),
            ],
            compiler_params=pltpu.CompilerParams(collective_id=0, has_side_effects=True),
            name="gated_conv",
        )(
            values,
            filter_taps,
            gate,
            bias.reshape(1, -1),
            jnp.asarray(fwd_hi),
            jnp.asarray(fwd_lo),
            jnp.asarray(inv_hi),
            jnp.asarray(inv_lo),
        )

    return jax.shard_map(
        body,
        mesh=mesh,
        in_specs=(P("ctx", "chan"), P("ctx", ("chan", "lag")), P("chan"), P("ctx", "chan")),
        out_specs=P("ctx", ("chan", "lag")),
        check_vma=False,
    )
```

```python
import functools
import math

import jax
import jax.numpy as jnp
import numpy as np
from jax import lax
from jax.experimental import pallas as pl
from jax.experimental.pallas import tpu as pltpu
from jax.sharding import PartitionSpec as P

MESH = pl.DeviceIdType.MESH
LANES = 128
HALF = 64
SIDE = 4


def halves(table):
    upper = table.astype(jnp.bfloat16)
    lower = (table - upper.astype(np.float64)).astype(jnp.bfloat16)
    return upper, lower


def tables(rows):
    length = 2 * rows
    order = np.arange(rows)
    freq = np.where(order < rows // 2, 2 * order, 2 * (order - rows // 2) + 1)
    token = np.arange(rows)
    angle = 2.0 * math.pi * ((freq[:, None] * token[None, :]) % length) / length
    alternate = np.where(token % 2 == 0, 1.0, -1.0)
    real, imag = np.cos(angle), -np.sin(angle)
    imag[0] = alternate
    weight = np.where(order == 0, 1.0, 2.0) / length
    back_real = (real * weight[:, None]).T
    back_imag = (imag * weight[:, None]).T
    back_imag[:, 0] = -alternate / length
    forward = np.concatenate([real, imag], axis=0)
    backward = np.concatenate([back_real, back_imag], axis=1)
    return halves(forward), halves(backward)


def hops(offset):
    return sum(min(part, SIDE - part) for part in divmod(offset, SIDE))


def peer_of(me, offset, count):
    dz, dy = divmod(offset, SIDE)
    z, y = me // SIDE, me % SIDE
    return ((z + dz) % (count // SIDE)) * SIDE + (y + dy) % SIDE


def kernel(
    count,
    values_hbm,
    taps_hbm,
    gate_hbm,
    bias_hbm,
    fwd_hbm,
    inv_hbm,
    out_ref,
    vbuf,
    tbuf,
    gbuf,
    bbuf,
    fwd,
    inv,
    packed,
    blocks,
    spec,
    turned,
    last,
    total,
    ret_send,
    ret_recv,
    load_sem,
    send_sem,
    recv_sem,
    back_send_sem,
    back_recv_sem,
):
    me = lax.axis_index("ctx")
    lag = lax.axis_index("lag")
    rows, share = vbuf.shape
    half_rows = rows // 2
    tiles = share // LANES
    middle = count // 2
    offsets = sorted(range(1, count), key=lambda o: -hops(o))

    barrier = pltpu.get_barrier_semaphore()
    for offset in offsets:
        pl.semaphore_signal(
            barrier, inc=1, device_id={"ctx": peer_of(me, offset, count)}, device_id_type=MESH
        )

    columns = pl.ds(pl.multiple_of(lag * share, share), share)
    loads = [
        pltpu.make_async_copy(src, dst, load_sem.at[i])
        for i, (src, dst) in enumerate(
            [
                (taps_hbm.at[:, columns], tbuf),
                (values_hbm.at[:, columns], vbuf),
                (fwd_hbm, fwd),
                (inv_hbm, inv),
                (bias_hbm.at[:, columns], bbuf),
                (gate_hbm, gbuf),
            ]
        )
    ]
    for load in loads:
        load.start()
    loads[0].wait()
    loads[1].wait()

    lower = lax.broadcasted_iota(jnp.int32, (rows, LANES), 1) < HALF
    for tile in range(tiles):
        lanes = slice(tile * LANES, (tile + 1) * LANES)
        value = vbuf[:, lanes].astype(jnp.float32)
        tap = pltpu.roll(tbuf[:, lanes].astype(jnp.float32), HALF, 1)
        packed[2 * tile] = jnp.where(lower, value, tap).astype(jnp.bfloat16)
        packed[2 * tile + 1] = jnp.where(lower, tap, value).astype(jnp.bfloat16)
    blocks[me] = packed[me]
    for load in loads[2:]:
        load.wait()

    pl.semaphore_wait(barrier, count - 1)
    sends = []
    for i, offset in enumerate(offsets):
        peer = peer_of(me, offset, count)
        copy = pltpu.make_async_remote_copy(
            src_ref=packed.at[peer],
            dst_ref=blocks.at[me],
            send_sem=send_sem.at[i],
            recv_sem=recv_sem.at[me],
            device_id={"ctx": peer},
            device_id_type=MESH,
        )
        copy.start()
        sends.append(copy)

    def arrival(buffer, sem, source):
        @pl.when(me != source)
        def _():
            pltpu.make_async_remote_copy(
                src_ref=buffer.at[source],
                dst_ref=buffer.at[source],
                send_sem=send_sem.at[0],
                recv_sem=sem.at[source],
                device_id={"ctx": source},
                device_id_type=MESH,
            ).wait_recv()

    def transform(members):
        for block in members:
            arrival(blocks, recv_sem, block)
        for block in members:
            both = jnp.dot(fwd[...], blocks[block], preferred_element_type=jnp.float32)
            spectrum = both[: 2 * rows] + both[2 * rows :]
            spec[block] = spectrum
            if block < middle:
                turned[block] = pltpu.roll(spectrum, HALF, 1)

    sub = lax.broadcasted_iota(jnp.int32, (8, LANES), 0)

    def products(outputs):
        def group(step, carry):
            sign = jnp.where(step < rows // 32, 1.0, -1.0)
            parts = []
            for part in range(2):
                start = pl.multiple_of(step * 16 + part * 8, 8)
                real_rows = pl.ds(start, 8)
                imag_rows = pl.ds(pl.multiple_of(rows + start, 8), 8)
                mask = jnp.where(sub + start > 0, 1.0, 0.0)

                def triple(ref, block):
                    real, imag = ref[block, real_rows], ref[block, imag_rows]
                    return real, imag, real + imag

                acc = {}
                for a in range(min(middle, outputs.stop // 2 + 1)):
                    left = triple(turned, a)
                    for b in range(max(a, outputs.start - a), outputs.stop - a):
                        right = triple(spec, b)
                        if a == b:
                            right = tuple(0.5 * r for r in right)
                        terms = tuple(x * y for x, y in zip(left, right))
                        old = acc.get(a + b)
                        acc[a + b] = (
                            terms if old is None else tuple(x + y for x, y in zip(old, terms))
                        )
                mixed = []
                before = None
                if outputs.start:
                    before = (last[real_rows], last[imag_rows])
                for n in outputs:
                    first, second, third = acc[n]
                    now = (first - mask * second, mask * (third - first) - second)
                    if before is None:
                        mixed.append(now)
                    else:
                        mixed.append((now[0] + sign * before[0], now[1] + sign * before[1]))
                    before = now
                if outputs.stop < count:
                    last[real_rows] = before[0]
                    last[imag_rows] = before[1]
                parts.append(mixed)
            start = pl.multiple_of(step * 16, 16)
            for n, upper, under in zip(outputs, *parts):
                total[n, pl.ds(start, 16)] = jnp.concatenate(
                    [upper[0], under[0]], axis=0
                ).astype(jnp.bfloat16)
                total[n, pl.ds(pl.multiple_of(rows + start, 16), 16)] = jnp.concatenate(
                    [upper[1], under[1]], axis=0
                ).astype(jnp.bfloat16)
            return carry

        lax.fori_loop(0, rows // 16, group, 0)

    lower_half = lax.broadcasted_iota(jnp.int32, (half_rows, LANES), 1) < HALF

    def restore(block):
        both = jnp.dot(inv[...], total[block], preferred_element_type=jnp.float32)
        result = both[:rows] + both[rows:]
        top, bottom = result[:half_rows], result[half_rows:]
        kept = jnp.where(lower_half, top, bottom)
        moved = pltpu.roll(jnp.where(lower_half, bottom, top), HALF, 1)
        return (kept + moved).astype(jnp.bfloat16)

    def back(block):
        return pltpu.make_async_remote_copy(
            src_ref=ret_send.at[block],
            dst_ref=ret_recv.at[me],
            send_sem=back_send_sem.at[block],
            recv_sem=back_recv_sem.at[me],
            device_id={"ctx": block},
            device_id_type=MESH,
        )

    def finish(outputs):
        width = len(outputs)
        batch = 4
        for first in range(0, width, batch):
            members = [
                outputs.start + (me + first + k) % width for k in range(batch)
            ]
            for block in members:
                ret_send[block] = restore(block)
            for block in members:

                @pl.when(block != me)
                def _():
                    back(block).start()

    quarter = count // 4
    for q in range(4):
        transform(range(q * quarter, (q + 1) * quarter))
        if q == 1:
            products(range(0, middle))
            finish(range(0, middle))
        if q == 3:
            products(range(middle, count))
            finish(range(middle, count))
    ret_recv[me] = ret_send[me]
    for copy in sends:
        copy.wait_send()

    for tile in range(tiles):
        lanes = slice(tile * LANES, (tile + 1) * LANES)
        arrival(ret_recv, back_recv_sem, 2 * tile)
        arrival(ret_recv, back_recv_sem, 2 * tile + 1)
        even = ret_recv[2 * tile].astype(jnp.float32)
        odd = ret_recv[2 * tile + 1].astype(jnp.float32)
        top = jnp.where(lower_half, even, pltpu.roll(odd, HALF, 1))
        bottom = jnp.where(lower_half, pltpu.roll(even, HALF, 1), odd)
        skip = bbuf[:, lanes]
        for part, conv in ((slice(0, half_rows), top), (slice(half_rows, rows), bottom)):
            value = vbuf[part, lanes].astype(jnp.float32)
            gate = gbuf[part, lanes].astype(jnp.float32)
            out_ref[part, lanes] = (gate * (conv + skip * value)).astype(jnp.bfloat16)
    for block in range(count):

        @pl.when(block != me)
        def _():
            back(block).wait_send()


def solution(mesh):
    count = mesh.shape["ctx"]
    lag_count = mesh.shape["lag"]

    def body(values, gate, bias, filter_taps):
        rows = values.shape[0]
        share = values.shape[1] // lag_count
        forward, inverse = tables(rows)
        any_spec = pl.BlockSpec(memory_space=pltpu.HBM)
        bf16, f32 = jnp.bfloat16, jnp.float32
        return pl.pallas_call(
            functools.partial(kernel, count),
            out_shape=pltpu.VMEM((rows, share), bf16),
            in_specs=[any_spec] * 6,
            out_specs=pl.BlockSpec(memory_space=pltpu.VMEM),
            scratch_shapes=[
                pltpu.VMEM((rows, share), bf16),
                pltpu.VMEM((rows, share), bf16),
                pltpu.VMEM((rows, share), bf16),
                pltpu.VMEM((1, share), f32),
                pltpu.VMEM((4 * rows, rows), bf16),
                pltpu.VMEM((2 * rows, 2 * rows), bf16),
                pltpu.VMEM((count, rows, LANES), bf16),
                pltpu.VMEM((count, rows, LANES), bf16),
                pltpu.VMEM((count, 2 * rows, LANES), f32),
                pltpu.VMEM((count // 2, 2 * rows, LANES), f32),
                pltpu.VMEM((2 * rows, LANES), f32),
                pltpu.VMEM((count, 2 * rows, LANES), bf16),
                pltpu.VMEM((count, rows // 2, LANES), bf16),
                pltpu.VMEM((count, rows // 2, LANES), bf16),
                pltpu.SemaphoreType.DMA((6,)),
                pltpu.SemaphoreType.DMA((count,)),
                pltpu.SemaphoreType.DMA((count,)),
                pltpu.SemaphoreType.DMA((count,)),
                pltpu.SemaphoreType.DMA((count,)),
            ],
            compiler_params=pltpu.CompilerParams(
                collective_id=0, has_side_effects=True, vmem_limit_bytes=60 * 2**20
            ),
            name="gated_conv",
        )(
            values,
            filter_taps,
            gate,
            bias.reshape(1, -1),
            jnp.asarray(np.concatenate(forward, axis=0)),
            jnp.asarray(np.concatenate(inverse, axis=0)),
        )

    return jax.shard_map(
        body,
        mesh=mesh,
        in_specs=(P("ctx", "chan"), P("ctx", ("chan", "lag")), P("chan"), P("ctx", "chan")),
        out_specs=P("ctx", ("chan", "lag")),
        check_vma=False,
    )
```

```python
import functools
import math

import jax
import jax.numpy as jnp
import numpy as np
from jax import lax
from jax.experimental import pallas as pl
from jax.experimental.pallas import tpu as pltpu
from jax.sharding import PartitionSpec as P

MESH = pl.DeviceIdType.MESH
LANES = 128
HALF = 64
SIDE = 4


def halves(table):
    upper = table.astype(jnp.bfloat16)
    lower = (table - upper.astype(np.float64)).astype(jnp.bfloat16)
    return upper, lower


def tables(rows):
    length = 2 * rows
    order = np.arange(rows)
    freq = np.where(order < rows // 2, 2 * order, 2 * (order - rows // 2) + 1)
    token = np.arange(rows)
    angle = 2.0 * math.pi * ((freq[:, None] * token[None, :]) % length) / length
    alternate = np.where(token % 2 == 0, 1.0, -1.0)
    real, imag = np.cos(angle), -np.sin(angle)
    imag[0] = alternate
    weight = np.where(order == 0, 1.0, 2.0) / length
    back_real = (real * weight[:, None]).T
    back_imag = (imag * weight[:, None]).T
    back_imag[:, 0] = -alternate / length
    forward = np.concatenate([real, imag], axis=0)
    backward = np.concatenate([back_real, back_imag], axis=1)
    return halves(forward), halves(backward)


OFFSETS = (6, 9, 14, 11, 10, 5, 15, 7, 13, 2, 8, 1, 4, 3, 12)


def peer_of(me, offset, count):
    dz, dy = divmod(offset, SIDE)
    row = (me + dz * SIDE) & (count - SIDE) if dz else me & (count - SIDE)
    column = (me + dy) & (SIDE - 1) if dy else me & (SIDE - 1)
    return row + column


def kernel(
    count,
    values_hbm,
    taps_hbm,
    gate_hbm,
    bias_hbm,
    fwd_hbm,
    inv_hbm,
    out_ref,
    vbuf,
    tbuf,
    gbuf,
    bbuf,
    fwd,
    inv,
    packed,
    blocks,
    spec,
    turned,
    last,
    partial,
    total,
    ret_send,
    ret_recv,
    load_sem,
    send_sem,
    recv_sem,
    back_send_sem,
    back_recv_sem,
):
    me = lax.axis_index("ctx")
    lag = lax.axis_index("lag")
    rows, share = vbuf.shape
    half_rows = rows // 2
    tiles = share // LANES
    middle = count // 2
    quarter = count // 4
    offsets = list(OFFSETS)

    columns = pl.ds(pl.multiple_of(lag * share, share), share)
    loads = [
        pltpu.make_async_copy(src, dst, load_sem.at[i])
        for i, (src, dst) in enumerate(
            [
                (taps_hbm.at[:, columns], tbuf),
                (values_hbm.at[:, columns], vbuf),
                (fwd_hbm, fwd),
                (inv_hbm, inv),
                (bias_hbm.at[:, columns], bbuf),
                (gate_hbm, gbuf),
            ]
        )
    ]
    for load in loads[:2]:
        load.start()
    barrier = pltpu.get_barrier_semaphore()
    for offset in offsets:
        pl.semaphore_signal(
            barrier, inc=1, device_id={"ctx": peer_of(me, offset, count)}, device_id_type=MESH
        )
    for load in loads[2:]:
        load.start()
    loads[0].wait()
    loads[1].wait()

    lower = lax.broadcasted_iota(jnp.int32, (rows, LANES), 1) < HALF
    for tile in range(tiles):
        lanes = slice(tile * LANES, (tile + 1) * LANES)
        value = vbuf[:, lanes].astype(jnp.float32)
        tap = pltpu.roll(tbuf[:, lanes].astype(jnp.float32), HALF, 1)
        packed[2 * tile] = jnp.where(lower, value, tap).astype(jnp.bfloat16)
        packed[2 * tile + 1] = jnp.where(lower, tap, value).astype(jnp.bfloat16)
    blocks[me] = packed[me]
    for load in loads[2:]:
        load.wait()

    pl.semaphore_wait(barrier, count - 1)
    sends = []
    for i, offset in enumerate(offsets):
        peer = peer_of(me, offset, count)
        copy = pltpu.make_async_remote_copy(
            src_ref=packed.at[peer],
            dst_ref=blocks.at[me],
            send_sem=send_sem.at[i],
            recv_sem=recv_sem.at[me],
            device_id={"ctx": peer},
            device_id_type=MESH,
        )
        copy.start()
        sends.append(copy)

    def arrival(buffer, sem, source):
        @pl.when(me != source)
        def _():
            pltpu.make_async_remote_copy(
                src_ref=buffer.at[source],
                dst_ref=buffer.at[source],
                send_sem=send_sem.at[0],
                recv_sem=sem.at[source],
                device_id={"ctx": source},
                device_id_type=MESH,
            ).wait_recv()

    def transform(members):
        for block in members:
            arrival(blocks, recv_sem, block)
        for block in members:
            both = jnp.dot(fwd[...], blocks[block], preferred_element_type=jnp.float32)
            spectrum = both[: 2 * rows] + both[2 * rows :]
            spec[block] = spectrum
            if block < middle:
                turned[block] = pltpu.roll(spectrum, HALF, 1)

    sub = lax.broadcasted_iota(jnp.int32, (8, LANES), 0)

    def products(stage):
        members = range(stage * quarter, (stage + 1) * quarter)
        pairs = [(a, b) for b in members for a in range(min(b, count - 1 - b) + 1)]
        touched = sorted({a + b for a, b in pairs} | set(members))
        began = {
            a + b for b in range(members.start) for a in range(min(b, count - 1 - b) + 1)
        }

        def group(step, carry):
            sign = jnp.where(step < rows // 32, 1.0, -1.0)
            parts = []
            for part in range(2):
                start = pl.multiple_of(step * 16 + part * 8, 8)
                real_rows = pl.ds(start, 8)
                imag_rows = pl.ds(pl.multiple_of(rows + start, 8), 8)
                mask = jnp.where(sub + start > 0, 1.0, 0.0)

                def triple(ref, block):
                    real, imag = ref[block, real_rows], ref[block, imag_rows]
                    return real, imag, real + imag

                acc = {}
                for n in touched:
                    if n in began:
                        acc[n] = tuple(partial[n, k, real_rows] for k in range(3))
                right = {b: triple(spec, b) for b in members}
                for a in range(max(a for a, _ in pairs) + 1):
                    left = triple(turned, a)
                    for b in members:
                        if (a, b) not in pairs:
                            continue
                        other = right[b] if a != b else tuple(0.5 * r for r in right[b])
                        terms = tuple(x * y for x, y in zip(left, other))
                        old = acc.get(a + b)
                        acc[a + b] = (
                            terms if old is None else tuple(x + y for x, y in zip(old, terms))
                        )
                for n in touched:
                    if n >= members.stop:
                        for k in range(3):
                            partial[n, k, real_rows] = acc[n][k]
                mixed = []
                before = (last[real_rows], last[imag_rows]) if stage else None
                for n in members:
                    first, second, third = acc[n]
                    now = (first - mask * second, mask * (third - first) - second)
                    if before is None:
                        mixed.append(now)
                    else:
                        mixed.append((now[0] + sign * before[0], now[1] + sign * before[1]))
                    before = now
                if members.stop < count:
                    last[real_rows] = before[0]
                    last[imag_rows] = before[1]
                parts.append(mixed)
            start = pl.multiple_of(step * 16, 16)
            for n, upper, under in zip(members, *parts):
                total[n, pl.ds(start, 16)] = jnp.concatenate(
                    [upper[0], under[0]], axis=0
                ).astype(jnp.bfloat16)
                total[n, pl.ds(pl.multiple_of(rows + start, 16), 16)] = jnp.concatenate(
                    [upper[1], under[1]], axis=0
                ).astype(jnp.bfloat16)
            return carry

        lax.fori_loop(0, rows // 16, group, 0, unroll=True)

    lower_half = lax.broadcasted_iota(jnp.int32, (half_rows, LANES), 1) < HALF

    def restore(block):
        both = jnp.dot(inv[...], total[block], preferred_element_type=jnp.float32)
        result = both[:rows] + both[rows:]
        top, bottom = result[:half_rows], result[half_rows:]
        kept = jnp.where(lower_half, top, bottom)
        moved = pltpu.roll(jnp.where(lower_half, bottom, top), HALF, 1)
        return (kept + moved).astype(jnp.bfloat16)

    def back(block):
        return pltpu.make_async_remote_copy(
            src_ref=ret_send.at[block],
            dst_ref=ret_recv.at[me],
            send_sem=back_send_sem.at[block],
            recv_sem=back_recv_sem.at[me],
            device_id={"ctx": block},
            device_id_type=MESH,
        )

    def finish(stage):
        members = [stage * quarter + ((me + k) & (quarter - 1)) for k in range(quarter)]
        for block in members:
            ret_send[block] = restore(block)
        for block in members:

            @pl.when(block != me)
            def _():
                back(block).start()

    for stage in range(4):
        transform(range(stage * quarter, (stage + 1) * quarter))
        products(stage)
        finish(stage)
    ret_recv[me] = ret_send[me]
    for copy in sends:
        copy.wait_send()

    for tile in range(tiles):
        lanes = slice(tile * LANES, (tile + 1) * LANES)
        arrival(ret_recv, back_recv_sem, 2 * tile)
        arrival(ret_recv, back_recv_sem, 2 * tile + 1)
        even = ret_recv[2 * tile].astype(jnp.float32)
        odd = ret_recv[2 * tile + 1].astype(jnp.float32)
        top = jnp.where(lower_half, even, pltpu.roll(odd, HALF, 1))
        bottom = jnp.where(lower_half, pltpu.roll(even, HALF, 1), odd)
        skip = bbuf[:, lanes]
        for part, conv in ((slice(0, half_rows), top), (slice(half_rows, rows), bottom)):
            value = vbuf[part, lanes].astype(jnp.float32)
            gate = gbuf[part, lanes].astype(jnp.float32)
            out_ref[part, lanes] = (gate * (conv + skip * value)).astype(jnp.bfloat16)
    for block in range(count):

        @pl.when(block != me)
        def _():
            back(block).wait_send()


def solution(mesh):
    count = mesh.shape["ctx"]
    lag_count = mesh.shape["lag"]

    def body(values, gate, bias, filter_taps):
        rows = values.shape[0]
        share = values.shape[1] // lag_count
        forward, inverse = tables(rows)
        any_spec = pl.BlockSpec(memory_space=pltpu.HBM)
        bf16, f32 = jnp.bfloat16, jnp.float32
        return pl.pallas_call(
            functools.partial(kernel, count),
            out_shape=pltpu.VMEM((rows, share), bf16),
            in_specs=[any_spec] * 6,
            out_specs=pl.BlockSpec(memory_space=pltpu.VMEM),
            scratch_shapes=[
                pltpu.VMEM((rows, share), bf16),
                pltpu.VMEM((rows, share), bf16),
                pltpu.VMEM((rows, share), bf16),
                pltpu.VMEM((1, share), f32),
                pltpu.VMEM((4 * rows, rows), bf16),
                pltpu.VMEM((2 * rows, 2 * rows), bf16),
                pltpu.VMEM((count, rows, LANES), bf16),
                pltpu.VMEM((count, rows, LANES), bf16),
                pltpu.VMEM((count, 2 * rows, LANES), f32),
                pltpu.VMEM((count // 2, 2 * rows, LANES), f32),
                pltpu.VMEM((2 * rows, LANES), f32),
                pltpu.VMEM((count, 3, rows, LANES), f32),
                pltpu.VMEM((count, 2 * rows, LANES), bf16),
                pltpu.VMEM((count, rows // 2, LANES), bf16),
                pltpu.VMEM((count, rows // 2, LANES), bf16),
                pltpu.SemaphoreType.DMA((6,)),
                pltpu.SemaphoreType.DMA((count,)),
                pltpu.SemaphoreType.DMA((count,)),
                pltpu.SemaphoreType.DMA((count,)),
                pltpu.SemaphoreType.DMA((count,)),
            ],
            compiler_params=pltpu.CompilerParams(
                collective_id=0, has_side_effects=True, vmem_limit_bytes=60 * 2**20
            ),
            name="gated_conv",
        )(
            values,
            filter_taps,
            gate,
            bias.reshape(1, -1),
            jnp.asarray(np.concatenate(forward, axis=0)),
            jnp.asarray(np.concatenate(inverse, axis=0)),
        )

    return jax.shard_map(
        body,
        mesh=mesh,
        in_specs=(P("ctx", "chan"), P("ctx", ("chan", "lag")), P("chan"), P("ctx", "chan")),
        out_specs=P("ctx", ("chan", "lag")),
        check_vma=False,
    )
```

```python
import functools
import math

import jax
import jax.numpy as jnp
import numpy as np
from jax import lax
from jax.experimental import pallas as pl
from jax.experimental.pallas import tpu as pltpu
from jax.sharding import PartitionSpec as P

MESH = pl.DeviceIdType.MESH
LANES = 128
HALF = 64


def halves(table):
    upper = table.astype(jnp.bfloat16)
    lower = (table - upper.astype(np.float64)).astype(jnp.bfloat16)
    return upper, lower


def tables(rows):
    length = 2 * rows
    order = np.arange(rows)
    freq = np.where(order < rows // 2, 2 * order, 2 * (order - rows // 2) + 1)
    token = np.arange(rows)
    angle = 2.0 * math.pi * ((freq[:, None] * token[None, :]) % length) / length
    alternate = np.where(token % 2 == 0, 1.0, -1.0)
    real, imag = np.cos(angle), -np.sin(angle)
    imag[0] = alternate
    weight = np.where(order == 0, 1.0, 2.0) / length
    back_real = (real * weight[:, None]).T
    back_imag = (imag * weight[:, None]).T
    back_imag[:, 0] = -alternate / length
    forward = np.concatenate([real, imag], axis=0)
    backward = np.concatenate([back_real, back_imag], axis=1)
    return halves(forward), halves(backward)


MASKS = (10, 6, 9, 14, 11, 8, 2, 5, 15, 7, 13, 1, 4, 3, 12)


def kernel(
    count,
    values_hbm,
    taps_hbm,
    gate_hbm,
    bias_hbm,
    fwd_hbm,
    inv_hbm,
    out_ref,
    vbuf,
    tbuf,
    gbuf,
    bbuf,
    fwd,
    inv,
    packed,
    blocks,
    spec,
    turned,
    last,
    partial,
    total,
    ret_send,
    ret_recv,
    load_sem,
    send_sem,
    recv_sem,
    back_send_sem,
    back_recv_sem,
):
    me = lax.axis_index("ctx")
    lag = lax.axis_index("lag")
    rows, share = vbuf.shape
    half_rows = rows // 2
    tiles = share // LANES
    middle = count // 2
    quarter = count // 4
    peers = [me ^ mask for mask in MASKS]

    columns = pl.ds(pl.multiple_of(lag * share, share), share)
    loads = [
        pltpu.make_async_copy(src, dst, load_sem.at[i])
        for i, (src, dst) in enumerate(
            [
                (taps_hbm.at[:, columns], tbuf),
                (values_hbm.at[:, columns], vbuf),
                (fwd_hbm, fwd),
                (inv_hbm, inv),
                (bias_hbm.at[:, columns], bbuf),
                (gate_hbm, gbuf),
            ]
        )
    ]
    for load in loads[:2]:
        load.start()
    barrier = pltpu.get_barrier_semaphore()
    for peer in peers:
        pl.semaphore_signal(barrier, inc=1, device_id={"ctx": peer}, device_id_type=MESH)
    for load in loads[2:]:
        load.start()
    loads[0].wait()
    loads[1].wait()

    lower = lax.broadcasted_iota(jnp.int32, (rows, LANES), 1) < HALF
    for tile in range(tiles):
        lanes = slice(tile * LANES, (tile + 1) * LANES)
        value = vbuf[:, lanes].astype(jnp.float32)
        tap = pltpu.roll(tbuf[:, lanes].astype(jnp.float32), HALF, 1)
        packed[2 * tile] = jnp.where(lower, value, tap).astype(jnp.bfloat16)
        packed[2 * tile + 1] = jnp.where(lower, tap, value).astype(jnp.bfloat16)
    blocks[me] = packed[me]
    for load in loads[2:]:
        load.wait()

    pl.semaphore_wait(barrier, count - 1)

    def send(peer):
        return pltpu.make_async_remote_copy(
            src_ref=packed.at[peer],
            dst_ref=blocks.at[me],
            send_sem=send_sem.at[peer],
            recv_sem=recv_sem.at[me],
            device_id={"ctx": peer},
            device_id_type=MESH,
        )

    for peer in peers:
        send(peer).start()

    def arrival(buffer, sem, source):
        @pl.when(me != source)
        def _():
            pltpu.make_async_remote_copy(
                src_ref=buffer.at[source],
                dst_ref=buffer.at[source],
                send_sem=send_sem.at[0],
                recv_sem=sem.at[source],
                device_id={"ctx": source},
                device_id_type=MESH,
            ).wait_recv()

    def row_blocks(row):
        return range(row * quarter, (row + 1) * quarter)

    def transform(row):
        members = row_blocks(row)
        for block in members:
            arrival(blocks, recv_sem, block)
        for block in members[::2]:
            pair = jnp.concatenate([blocks[block], blocks[block + 1]], axis=1)
            both = jnp.dot(fwd[...], pair, preferred_element_type=jnp.float32)
            spectra = both[: 2 * rows] + both[2 * rows :]
            for k in range(2):
                spectrum = spectra[:, k * LANES : (k + 1) * LANES]
                spec[block + k] = spectrum
                if block < middle:
                    turned[block + k] = pltpu.roll(spectrum, HALF, 1)

    sub = lax.broadcasted_iota(jnp.int32, (8, LANES), 0)

    begun, closed = set(), []

    def products(pairs, close):
        closing = [n for row in close for n in range(row * quarter, (row + 1) * quarter)]
        touched = sorted({a + b for a, b in pairs} | set(closing))
        loaded = [n for n in touched if n in begun]
        first_close = not closed
        lefts = sorted({a for a, _ in pairs})
        rights = sorted({b for _, b in pairs})

        def group(step, carry):
            sign = jnp.where(step < rows // 32, 1.0, -1.0)
            parts = []
            for part in range(2):
                start = pl.multiple_of(step * 16 + part * 8, 8)
                real_rows = pl.ds(start, 8)
                imag_rows = pl.ds(pl.multiple_of(rows + start, 8), 8)
                mask = jnp.where(sub + start > 0, 1.0, 0.0)

                def triple(ref, block):
                    real, imag = ref[block, real_rows], ref[block, imag_rows]
                    return real, imag, real + imag

                acc = {}
                for n in loaded:
                    acc[n] = tuple(partial[n, k, real_rows] for k in range(3))
                right = {b: triple(spec, b) for b in rights}
                for a in lefts:
                    left = triple(turned, a)
                    for b in rights:
                        if (a, b) not in pairs:
                            continue
                        other = right[b] if a != b else tuple(0.5 * r for r in right[b])
                        terms = tuple(x * y for x, y in zip(left, other))
                        old = acc.get(a + b)
                        acc[a + b] = (
                            terms if old is None else tuple(x + y for x, y in zip(old, terms))
                        )
                for n in touched:
                    if n not in closing:
                        for k in range(3):
                            partial[n, k, real_rows] = acc[n][k]
                if not closing:
                    continue
                mixed = []
                before = None if first_close else (last[real_rows], last[imag_rows])
                for n in closing:
                    first, second, third = acc[n]
                    now = (first - mask * second, mask * (third - first) - second)
                    if before is None:
                        mixed.append(now)
                    else:
                        mixed.append((now[0] + sign * before[0], now[1] + sign * before[1]))
                    before = now
                if closing[-1] < count - 1:
                    last[real_rows] = before[0]
                    last[imag_rows] = before[1]
                parts.append(mixed)
            if not closing:
                return carry
            start = pl.multiple_of(step * 16, 16)
            for n, upper, under in zip(closing, *parts):
                total[n, pl.ds(start, 16)] = jnp.concatenate(
                    [upper[0], under[0]], axis=0
                ).astype(jnp.bfloat16)
                total[n, pl.ds(pl.multiple_of(rows + start, 16), 16)] = jnp.concatenate(
                    [upper[1], under[1]], axis=0
                ).astype(jnp.bfloat16)
            return carry

        lax.fori_loop(0, rows // 16, group, 0, unroll=True)
        begun.update(touched)
        closed.extend(closing)

    lower_half = lax.broadcasted_iota(jnp.int32, (half_rows, LANES), 1) < HALF

    def restore(first, second):
        pair = jnp.concatenate([total[first], total[second]], axis=1)
        both = jnp.dot(inv[...], pair, preferred_element_type=jnp.float32)
        results = both[:rows] + both[rows:]
        for k, block in enumerate((first, second)):
            result = results[:, k * LANES : (k + 1) * LANES]
            top, bottom = result[:half_rows], result[half_rows:]
            kept = jnp.where(lower_half, top, bottom)
            moved = pltpu.roll(jnp.where(lower_half, bottom, top), HALF, 1)
            ret_send[block] = (kept + moved).astype(jnp.bfloat16)

    def back(block):
        return pltpu.make_async_remote_copy(
            src_ref=ret_send.at[block],
            dst_ref=ret_recv.at[me],
            send_sem=back_send_sem.at[block],
            recv_sem=back_recv_sem.at[me],
            device_id={"ctx": block},
            device_id_type=MESH,
        )

    def finish(*groups):
        for members in groups:
            for first, second in zip(members[::2], members[1::2]):
                restore(first, second)
            for block in members:

                @pl.when(block != me)
                def _():
                    back(block).start()

    def pairs_of(left, right):
        return [
            (a, b)
            for a in row_blocks(left)
            for b in row_blocks(right)
            if a <= b and a + b < count
        ]

    transform(3)
    transform(2)
    transform(0)
    products(pairs_of(0, 0), [0])
    finish([0, 1, 3, 2])
    products(pairs_of(0, 2) + pairs_of(0, 3), [])
    transform(1)
    products(pairs_of(0, 1) + pairs_of(1, 1), [1])
    finish([4, 5, 7, 6])
    products(pairs_of(1, 2), [2])
    finish([8, 9, 11, 10])
    products([], [3])
    finish([12, 13, 15, 14])
    ret_recv[me] = ret_send[me]
    for peer in peers:
        send(peer).wait_send()

    for tile in range(tiles):
        lanes = slice(tile * LANES, (tile + 1) * LANES)
        arrival(ret_recv, back_recv_sem, 2 * tile)
        arrival(ret_recv, back_recv_sem, 2 * tile + 1)
        even = ret_recv[2 * tile].astype(jnp.float32)
        odd = ret_recv[2 * tile + 1].astype(jnp.float32)
        top = jnp.where(lower_half, even, pltpu.roll(odd, HALF, 1))
        bottom = jnp.where(lower_half, pltpu.roll(even, HALF, 1), odd)
        skip = bbuf[:, lanes]
        for part, conv in ((slice(0, half_rows), top), (slice(half_rows, rows), bottom)):
            value = vbuf[part, lanes].astype(jnp.float32)
            gate = gbuf[part, lanes].astype(jnp.float32)
            out_ref[part, lanes] = (gate * (conv + skip * value)).astype(jnp.bfloat16)
    for block in range(count):

        @pl.when(block != me)
        def _():
            back(block).wait_send()


def solution(mesh):
    count = mesh.shape["ctx"]
    lag_count = mesh.shape["lag"]

    def body(values, gate, bias, filter_taps):
        rows = values.shape[0]
        share = values.shape[1] // lag_count
        forward, inverse = tables(rows)
        any_spec = pl.BlockSpec(memory_space=pltpu.HBM)
        bf16, f32 = jnp.bfloat16, jnp.float32
        return pl.pallas_call(
            functools.partial(kernel, count),
            out_shape=pltpu.VMEM((rows, share), bf16),
            in_specs=[any_spec] * 6,
            out_specs=pl.BlockSpec(memory_space=pltpu.VMEM),
            scratch_shapes=[
                pltpu.VMEM((rows, share), bf16),
                pltpu.VMEM((rows, share), bf16),
                pltpu.VMEM((rows, share), bf16),
                pltpu.VMEM((1, share), f32),
                pltpu.VMEM((4 * rows, rows), bf16),
                pltpu.VMEM((2 * rows, 2 * rows), bf16),
                pltpu.VMEM((count, rows, LANES), bf16),
                pltpu.VMEM((count, rows, LANES), bf16),
                pltpu.VMEM((count, 2 * rows, LANES), f32),
                pltpu.VMEM((count // 2, 2 * rows, LANES), f32),
                pltpu.VMEM((2 * rows, LANES), f32),
                pltpu.VMEM((count, 3, rows, LANES), f32),
                pltpu.VMEM((count, 2 * rows, LANES), bf16),
                pltpu.VMEM((count, rows // 2, LANES), bf16),
                pltpu.VMEM((count, rows // 2, LANES), bf16),
                pltpu.SemaphoreType.DMA((6,)),
                pltpu.SemaphoreType.DMA((count,)),
                pltpu.SemaphoreType.DMA((count,)),
                pltpu.SemaphoreType.DMA((count,)),
                pltpu.SemaphoreType.DMA((count,)),
            ],
            compiler_params=pltpu.CompilerParams(
                collective_id=0, has_side_effects=True, vmem_limit_bytes=60 * 2**20
            ),
            name="gated_conv",
        )(
            values,
            filter_taps,
            gate,
            bias.reshape(1, -1),
            jnp.asarray(np.concatenate(forward, axis=0)),
            jnp.asarray(np.concatenate(inverse, axis=0)),
        )

    return jax.shard_map(
        body,
        mesh=mesh,
        in_specs=(P("ctx", "chan"), P("ctx", ("chan", "lag")), P("chan"), P("ctx", "chan")),
        out_specs=P("ctx", ("chan", "lag")),
        check_vma=False,
    )
```

```python
import functools
import math

import jax
import jax.numpy as jnp
import numpy as np
from jax import lax
from jax.experimental import pallas as pl
from jax.experimental.pallas import tpu as pltpu
from jax.sharding import PartitionSpec as P

MESH = pl.DeviceIdType.MESH
LANES = 128
HALF = 64


def halves(table):
    upper = table.astype(jnp.bfloat16)
    lower = (table - upper.astype(np.float64)).astype(jnp.bfloat16)
    return upper, lower


def tables(rows):
    length = 2 * rows
    order = np.arange(rows)
    freq = np.where(order < rows // 2, 2 * order, 2 * (order - rows // 2) + 1)
    token = np.arange(rows)
    angle = 2.0 * math.pi * ((freq[:, None] * token[None, :]) % length) / length
    alternate = np.where(token % 2 == 0, 1.0, -1.0)
    real, imag = np.cos(angle), -np.sin(angle)
    imag[0] = alternate
    weight = np.where(order == 0, 1.0, 2.0) / length
    back_real = (real * weight[:, None]).T
    back_imag = (imag * weight[:, None]).T
    back_imag[:, 0] = -alternate / length
    forward = np.concatenate([real, imag], axis=0)
    backward = np.concatenate([back_real, back_imag], axis=1)
    return halves(forward), halves(backward)


MASKS = (10, 6, 9, 14, 11, 8, 2, 5, 15, 7, 13, 1, 4, 3, 12)


def kernel(
    count,
    values_hbm,
    taps_hbm,
    gate_hbm,
    bias_hbm,
    fwd_hbm,
    inv_hbm,
    out_ref,
    vbuf,
    tbuf,
    gbuf,
    bbuf,
    fwd,
    inv,
    packed,
    blocks,
    spec,
    turned,
    last,
    partial,
    total,
    ret_send,
    ret_recv,
    load_sem,
    send_sem,
    recv_sem,
    back_send_sem,
    back_recv_sem,
):
    me = lax.axis_index("ctx")
    lag = lax.axis_index("lag")
    rows, share = vbuf.shape
    half_rows = rows // 2
    tiles = share // LANES
    middle = count // 2
    quarter = count // 4
    peers = [me ^ mask for mask in MASKS]

    barrier = pltpu.get_barrier_semaphore()
    for peer in peers:
        pl.semaphore_signal(barrier, inc=1, device_id={"ctx": peer}, device_id_type=MESH)

    columns = pl.ds(pl.multiple_of(lag * share, share), share)
    loads = [
        pltpu.make_async_copy(src, dst, load_sem.at[i])
        for i, (src, dst) in enumerate(
            [
                (taps_hbm.at[:, columns], tbuf),
                (values_hbm.at[:, columns], vbuf),
                (fwd_hbm, fwd),
                (inv_hbm, inv),
                (bias_hbm.at[:, columns], bbuf),
                (gate_hbm, gbuf),
            ]
        )
    ]
    for load in loads[:2]:
        load.start()
    for load in loads[2:]:
        load.start()
    loads[0].wait()
    loads[1].wait()

    lower = lax.broadcasted_iota(jnp.int32, (rows, LANES), 1) < HALF
    for tile in range(tiles):
        lanes = slice(tile * LANES, (tile + 1) * LANES)
        value = vbuf[:, lanes].astype(jnp.float32)
        tap = pltpu.roll(tbuf[:, lanes].astype(jnp.float32), HALF, 1)
        packed[2 * tile] = jnp.where(lower, value, tap).astype(jnp.bfloat16)
        packed[2 * tile + 1] = jnp.where(lower, tap, value).astype(jnp.bfloat16)
    blocks[me] = packed[me]
    for load in loads[2:]:
        load.wait()

    pl.semaphore_wait(barrier, count - 1)

    def send(peer):
        return pltpu.make_async_remote_copy(
            src_ref=packed.at[peer],
            dst_ref=blocks.at[me],
            send_sem=send_sem.at[peer],
            recv_sem=recv_sem.at[me],
            device_id={"ctx": peer},
            device_id_type=MESH,
        )

    for peer in peers:
        send(peer).start()

    def arrival(buffer, sem, source):
        @pl.when(me != source)
        def _():
            pltpu.make_async_remote_copy(
                src_ref=buffer.at[source],
                dst_ref=buffer.at[source],
                send_sem=send_sem.at[0],
                recv_sem=sem.at[source],
                device_id={"ctx": source},
                device_id_type=MESH,
            ).wait_recv()

    def row_blocks(row):
        return range(row * quarter, (row + 1) * quarter)

    def transform(row):
        members = row_blocks(row)
        for block in members:
            arrival(blocks, recv_sem, block)
        for block in members[::2]:
            pair = jnp.concatenate([blocks[block], blocks[block + 1]], axis=1)
            both = jnp.dot(fwd[...], pair, preferred_element_type=jnp.float32)
            spectra = both[: 2 * rows] + both[2 * rows :]
            for k in range(2):
                spectrum = spectra[:, k * LANES : (k + 1) * LANES]
                spec[block + k] = spectrum
                if block < middle:
                    turned[block + k] = pltpu.roll(spectrum, HALF, 1)

    sub = lax.broadcasted_iota(jnp.int32, (8, LANES), 0)

    begun, closed = set(), []

    def products(pairs, close):
        closing = [n for row in close for n in range(row * quarter, (row + 1) * quarter)]
        touched = sorted({a + b for a, b in pairs} | set(closing))
        loaded = [n for n in touched if n in begun]
        first_close = not closed
        lefts = sorted({a for a, _ in pairs})
        rights = sorted({b for _, b in pairs})

        def group(step, carry):
            sign = jnp.where(step < rows // 32, 1.0, -1.0)
            parts = []
            for part in range(2):
                start = pl.multiple_of(step * 16 + part * 8, 8)
                real_rows = pl.ds(start, 8)
                imag_rows = pl.ds(pl.multiple_of(rows + start, 8), 8)
                mask = jnp.where(sub + start > 0, 1.0, 0.0)

                def triple(ref, block):
                    real, imag = ref[block, real_rows], ref[block, imag_rows]
                    return real, imag, real + imag

                acc = {}
                for n in loaded:
                    acc[n] = tuple(partial[n, k, real_rows] for k in range(3))
                right = {b: triple(spec, b) for b in rights}
                for a in lefts:
                    left = triple(turned, a)
                    for b in rights:
                        if (a, b) not in pairs:
                            continue
                        other = right[b] if a != b else tuple(0.5 * r for r in right[b])
                        terms = tuple(x * y for x, y in zip(left, other))
                        old = acc.get(a + b)
                        acc[a + b] = (
                            terms if old is None else tuple(x + y for x, y in zip(old, terms))
                        )
                for n in touched:
                    if n not in closing:
                        for k in range(3):
                            partial[n, k, real_rows] = acc[n][k]
                if not closing:
                    continue
                mixed = []
                before = None if first_close else (last[real_rows], last[imag_rows])
                for n in closing:
                    first, second, third = acc[n]
                    now = (first - mask * second, mask * (third - first) - second)
                    if before is None:
                        mixed.append(now)
                    else:
                        mixed.append((now[0] + sign * before[0], now[1] + sign * before[1]))
                    before = now
                if closing[-1] < count - 1:
                    last[real_rows] = before[0]
                    last[imag_rows] = before[1]
                parts.append(mixed)
            if not closing:
                return carry
            start = pl.multiple_of(step * 16, 16)
            for n, upper, under in zip(closing, *parts):
                total[n, pl.ds(start, 16)] = jnp.concatenate(
                    [upper[0], under[0]], axis=0
                ).astype(jnp.bfloat16)
                total[n, pl.ds(pl.multiple_of(rows + start, 16), 16)] = jnp.concatenate(
                    [upper[1], under[1]], axis=0
                ).astype(jnp.bfloat16)
            return carry

        lax.fori_loop(0, rows // 16, group, 0, unroll=True)
        begun.update(touched)
        closed.extend(closing)

    lower_half = lax.broadcasted_iota(jnp.int32, (half_rows, LANES), 1) < HALF

    def restore(first, second):
        pair = jnp.concatenate([total[first], total[second]], axis=1)
        both = jnp.dot(inv[...], pair, preferred_element_type=jnp.float32)
        results = both
        for k, block in enumerate((first, second)):
            result = results[:, k * LANES : (k + 1) * LANES]
            top, bottom = result[:half_rows], result[half_rows:]
            kept = jnp.where(lower_half, top, bottom)
            moved = pltpu.roll(jnp.where(lower_half, bottom, top), HALF, 1)
            ret_send[block] = (kept + moved).astype(jnp.bfloat16)

    def back(block):
        return pltpu.make_async_remote_copy(
            src_ref=ret_send.at[block],
            dst_ref=ret_recv.at[me],
            send_sem=back_send_sem.at[block],
            recv_sem=back_recv_sem.at[me],
            device_id={"ctx": block},
            device_id_type=MESH,
        )

    def finish(*groups):
        for members in groups:
            for first, second in zip(members[::2], members[1::2]):
                restore(first, second)
            for block in members:

                @pl.when(block != me)
                def _():
                    back(block).start()

    def pairs_of(left, right):
        return [
            (a, b)
            for a in row_blocks(left)
            for b in row_blocks(right)
            if a <= b and a + b < count
        ]

    transform(3)
    transform(2)
    transform(0)
    products(pairs_of(0, 0), [0])
    finish([0, 1])
    products(pairs_of(0, 2) + pairs_of(0, 3), [])
    transform(1)
    products(pairs_of(0, 1) + pairs_of(1, 1), [1])
    finish([4, 5, 3, 2])
    products(pairs_of(1, 2), [2])
    finish([8, 9, 7, 6])
    products([], [3])
    finish([12, 13, 11, 10], [15, 14])
    ret_recv[me] = ret_send[me]
    for peer in peers:
        send(peer).wait_send()

    for tile in range(tiles):
        lanes = slice(tile * LANES, (tile + 1) * LANES)
        arrival(ret_recv, back_recv_sem, 2 * tile)
        arrival(ret_recv, back_recv_sem, 2 * tile + 1)
        even = ret_recv[2 * tile].astype(jnp.float32)
        odd = ret_recv[2 * tile + 1].astype(jnp.float32)
        top = jnp.where(lower_half, even, pltpu.roll(odd, HALF, 1))
        bottom = jnp.where(lower_half, pltpu.roll(even, HALF, 1), odd)
        skip = bbuf[:, lanes]
        for part, conv in ((slice(0, half_rows), top), (slice(half_rows, rows), bottom)):
            value = vbuf[part, lanes].astype(jnp.float32)
            gate = gbuf[part, lanes].astype(jnp.float32)
            out_ref[part, lanes] = (gate * (conv + skip * value)).astype(jnp.bfloat16)
    for block in range(count):

        @pl.when(block != me)
        def _():
            back(block).wait_send()


def solution(mesh):
    count = mesh.shape["ctx"]
    lag_count = mesh.shape["lag"]

    def body(values, gate, bias, filter_taps):
        rows = values.shape[0]
        share = values.shape[1] // lag_count
        forward, inverse = tables(rows)
        any_spec = pl.BlockSpec(memory_space=pltpu.HBM)
        bf16, f32 = jnp.bfloat16, jnp.float32
        return pl.pallas_call(
            functools.partial(kernel, count),
            out_shape=pltpu.VMEM((rows, share), bf16),
            in_specs=[any_spec] * 6,
            out_specs=pl.BlockSpec(memory_space=pltpu.VMEM),
            scratch_shapes=[
                pltpu.VMEM((rows, share), bf16),
                pltpu.VMEM((rows, share), bf16),
                pltpu.VMEM((rows, share), bf16),
                pltpu.VMEM((1, share), f32),
                pltpu.VMEM((4 * rows, rows), bf16),
                pltpu.VMEM((rows, 2 * rows), bf16),
                pltpu.VMEM((count, rows, LANES), bf16),
                pltpu.VMEM((count, rows, LANES), bf16),
                pltpu.VMEM((count, 2 * rows, LANES), f32),
                pltpu.VMEM((count // 2, 2 * rows, LANES), f32),
                pltpu.VMEM((2 * rows, LANES), f32),
                pltpu.VMEM((count, 3, rows, LANES), f32),
                pltpu.VMEM((count, 2 * rows, LANES), bf16),
                pltpu.VMEM((count, rows // 2, LANES), bf16),
                pltpu.VMEM((count, rows // 2, LANES), bf16),
                pltpu.SemaphoreType.DMA((6,)),
                pltpu.SemaphoreType.DMA((count,)),
                pltpu.SemaphoreType.DMA((count,)),
                pltpu.SemaphoreType.DMA((count,)),
                pltpu.SemaphoreType.DMA((count,)),
            ],
            compiler_params=pltpu.CompilerParams(
                collective_id=0, has_side_effects=True, vmem_limit_bytes=60 * 2**20
            ),
            name="gated_conv",
        )(
            values,
            filter_taps,
            gate,
            bias.reshape(1, -1),
            jnp.asarray(np.concatenate(forward, axis=0)),
            jnp.asarray(inverse[0]),
        )

    return jax.shard_map(
        body,
        mesh=mesh,
        in_specs=(P("ctx", "chan"), P("ctx", ("chan", "lag")), P("chan"), P("ctx", "chan")),
        out_specs=P("ctx", ("chan", "lag")),
        check_vma=False,
    )
```

```python
import functools
import math

import jax
import jax.numpy as jnp
import numpy as np
from jax import lax
from jax.experimental import pallas as pl
from jax.experimental.pallas import tpu as pltpu
from jax.sharding import PartitionSpec as P

MESH = pl.DeviceIdType.MESH
LANES = 128
HALF = 64


def halves(table):
    upper = table.astype(jnp.bfloat16)
    lower = (table - upper.astype(np.float64)).astype(jnp.bfloat16)
    return upper, lower


def tables(rows):
    length = 2 * rows
    order = np.arange(rows)
    freq = np.where(order < rows // 2, 2 * order, 2 * (order - rows // 2) + 1)
    token = np.arange(rows)
    angle = 2.0 * math.pi * ((freq[:, None] * token[None, :]) % length) / length
    alternate = np.where(token % 2 == 0, 1.0, -1.0)
    real, imag = np.cos(angle), -np.sin(angle)
    imag[0] = alternate
    weight = np.where(order == 0, 1.0, 2.0) / length
    back_real = (real * weight[:, None]).T
    back_imag = (imag * weight[:, None]).T
    back_imag[:, 0] = -alternate / length
    forward = np.concatenate([real, imag], axis=0)
    backward = np.concatenate([back_real, back_imag], axis=1)
    return halves(forward), halves(backward)


MASKS = (10, 6, 9, 14, 11, 8, 2, 5, 15, 7, 13, 1, 4, 3, 12)


def kernel(
    count,
    values_hbm,
    taps_hbm,
    gate_hbm,
    bias_hbm,
    fwd_hbm,
    inv_hbm,
    out_ref,
    vbuf,
    tbuf,
    gbuf,
    bbuf,
    fwd,
    inv,
    packed,
    blocks,
    spec,
    turned,
    last,
    partial,
    total,
    ret_send,
    ret_recv,
    load_sem,
    send_sem,
    recv_sem,
    back_send_sem,
    back_recv_sem,
):
    me = lax.axis_index("ctx")
    lag = lax.axis_index("lag")
    rows, share = vbuf.shape
    half_rows = rows // 2
    tiles = share // LANES
    middle = count // 2
    quarter = count // 4
    peers = [me ^ mask for mask in MASKS]

    barrier = pltpu.get_barrier_semaphore()
    for peer in peers:
        pl.semaphore_signal(barrier, inc=1, device_id={"ctx": peer}, device_id_type=MESH)

    columns = pl.ds(pl.multiple_of(lag * share, share), share)
    loads = [
        pltpu.make_async_copy(src, dst, load_sem.at[i])
        for i, (src, dst) in enumerate(
            [
                (taps_hbm.at[:, columns], tbuf),
                (values_hbm.at[:, columns], vbuf),
                (fwd_hbm, fwd),
                (inv_hbm, inv),
                (bias_hbm.at[:, columns], bbuf),
                (gate_hbm, gbuf),
            ]
        )
    ]
    for load in loads[:2]:
        load.start()
    for load in loads[2:]:
        load.start()
    loads[0].wait()
    loads[1].wait()

    lower = lax.broadcasted_iota(jnp.int32, (rows, LANES), 1) < HALF
    for tile in range(tiles):
        lanes = slice(tile * LANES, (tile + 1) * LANES)
        value = vbuf[:, lanes].astype(jnp.float32)
        tap = pltpu.roll(tbuf[:, lanes].astype(jnp.float32), HALF, 1)
        packed[2 * tile] = jnp.where(lower, value, tap).astype(jnp.bfloat16)
        packed[2 * tile + 1] = jnp.where(lower, tap, value).astype(jnp.bfloat16)
    blocks[me] = packed[me]
    for load in loads[2:]:
        load.wait()

    pl.semaphore_wait(barrier, count - 1)

    def send(peer):
        return pltpu.make_async_remote_copy(
            src_ref=packed.at[peer],
            dst_ref=blocks.at[me],
            send_sem=send_sem.at[peer],
            recv_sem=recv_sem.at[me],
            device_id={"ctx": peer},
            device_id_type=MESH,
        )

    for peer in peers:
        send(peer).start()

    def arrival(buffer, sem, source):
        @pl.when(me != source)
        def _():
            pltpu.make_async_remote_copy(
                src_ref=buffer.at[source],
                dst_ref=buffer.at[source],
                send_sem=send_sem.at[0],
                recv_sem=sem.at[source],
                device_id={"ctx": source},
                device_id_type=MESH,
            ).wait_recv()

    def row_blocks(row):
        return range(row * quarter, (row + 1) * quarter)

    def transform(row):
        members = row_blocks(row)
        for block in members:
            arrival(blocks, recv_sem, block)
        for block in members[::2]:
            pair = jnp.concatenate([blocks[block], blocks[block + 1]], axis=1)
            both = jnp.dot(fwd[...], pair, preferred_element_type=jnp.float32)
            spectra = both[: 2 * rows] + both[2 * rows :]
            for k in range(2):
                spectrum = spectra[:, k * LANES : (k + 1) * LANES]
                spec[block + k] = spectrum
                if block < middle:
                    turned[block + k] = pltpu.roll(spectrum, HALF, 1)

    sub = lax.broadcasted_iota(jnp.int32, (8, LANES), 0)

    begun, closed = set(), []

    def products(pairs, close):
        closing = [n for row in close for n in range(row * quarter, (row + 1) * quarter)]
        touched = sorted({a + b for a, b in pairs} | set(closing))
        loaded = [n for n in touched if n in begun]
        first_close = not closed
        lefts = sorted({a for a, _ in pairs})
        rights = sorted({b for _, b in pairs})

        def group(step, carry):
            sign = jnp.where(step < rows // 32, 1.0, -1.0)
            parts = []
            for part in range(2):
                start = pl.multiple_of(step * 16 + part * 8, 8)
                real_rows = pl.ds(start, 8)
                imag_rows = pl.ds(pl.multiple_of(rows + start, 8), 8)
                mask = jnp.where(sub + start > 0, 1.0, 0.0)

                def triple(ref, block):
                    real, imag = ref[block, real_rows], ref[block, imag_rows]
                    return real, imag, real + imag

                acc = {}
                for n in loaded:
                    acc[n] = tuple(partial[n, k, real_rows] for k in range(3))
                right = {b: triple(spec, b) for b in rights}
                for a in lefts:
                    left = triple(turned, a)
                    for b in rights:
                        if (a, b) not in pairs:
                            continue
                        other = right[b] if a != b else tuple(0.5 * r for r in right[b])
                        terms = tuple(x * y for x, y in zip(left, other))
                        old = acc.get(a + b)
                        acc[a + b] = (
                            terms if old is None else tuple(x + y for x, y in zip(old, terms))
                        )
                for n in touched:
                    if n not in closing:
                        for k in range(3):
                            partial[n, k, real_rows] = acc[n][k]
                if not closing:
                    continue
                mixed = []
                before = None if first_close else (last[real_rows], last[imag_rows])
                for n in closing:
                    first, second, third = acc[n]
                    now = (first - mask * second, mask * (third - first) - second)
                    if before is None:
                        mixed.append(now)
                    else:
                        mixed.append((now[0] + sign * before[0], now[1] + sign * before[1]))
                    before = now
                if closing[-1] < count - 1:
                    last[real_rows] = before[0]
                    last[imag_rows] = before[1]
                parts.append(mixed)
            if not closing:
                return carry
            start = pl.multiple_of(step * 16, 16)
            for n, upper, under in zip(closing, *parts):
                total[n, pl.ds(start, 16)] = jnp.concatenate(
                    [upper[0], under[0]], axis=0
                ).astype(jnp.bfloat16)
                total[n, pl.ds(pl.multiple_of(rows + start, 16), 16)] = jnp.concatenate(
                    [upper[1], under[1]], axis=0
                ).astype(jnp.bfloat16)
            return carry

        lax.fori_loop(0, rows // 16, group, 0, unroll=True)
        begun.update(touched)
        closed.extend(closing)

    lower_half = lax.broadcasted_iota(jnp.int32, (half_rows, LANES), 1) < HALF

    def restore(first, second):
        pair = jnp.concatenate([total[first], total[second]], axis=1)
        both = jnp.dot(inv[...], pair, preferred_element_type=jnp.float32)
        results = both
        for k, block in enumerate((first, second)):
            result = results[:, k * LANES : (k + 1) * LANES]
            top, bottom = result[:half_rows], result[half_rows:]
            kept = jnp.where(lower_half, top, bottom)
            moved = pltpu.roll(jnp.where(lower_half, bottom, top), HALF, 1)
            ret_send[block] = (kept + moved).astype(jnp.bfloat16)

    def back(block):
        return pltpu.make_async_remote_copy(
            src_ref=ret_send.at[block],
            dst_ref=ret_recv.at[me],
            send_sem=back_send_sem.at[block],
            recv_sem=back_recv_sem.at[me],
            device_id={"ctx": block},
            device_id_type=MESH,
        )

    def finish(*groups):
        for members in groups:
            for first, second in zip(members[::2], members[1::2]):
                restore(first, second)
            for block in members:

                @pl.when(block != me)
                def _():
                    back(block).start()

    def pairs_of(left, right):
        return [
            (a, b)
            for a in row_blocks(left)
            for b in row_blocks(right)
            if a <= b and a + b < count
        ]

    transform(3)
    transform(2)
    transform(0)
    products(pairs_of(0, 0), [0])
    finish([0, 1])
    products(pairs_of(0, 2) + pairs_of(0, 3), [])
    transform(1)
    products(pairs_of(0, 1) + pairs_of(1, 1), [1])
    finish([4, 5, 3, 2])
    products(pairs_of(1, 2), [2])
    finish([8, 9, 7, 6])
    products([], [3])
    finish([12, 13, 11, 10], [15, 14])
    ret_recv[me] = ret_send[me]
    for peer in peers:
        send(peer).wait_send()

    for step in (0, 2, 1, 6, 3, 4, 7, 5):
        tile = (me // 2) ^ step
        lanes = pl.ds(pl.multiple_of(tile * LANES, LANES), LANES)
        arrival(ret_recv, back_recv_sem, 2 * tile)
        arrival(ret_recv, back_recv_sem, 2 * tile + 1)
        even = ret_recv[2 * tile].astype(jnp.float32)
        odd = ret_recv[2 * tile + 1].astype(jnp.float32)
        top = jnp.where(lower_half, even, pltpu.roll(odd, HALF, 1))
        bottom = jnp.where(lower_half, pltpu.roll(even, HALF, 1), odd)
        skip = bbuf[:, lanes]
        for part, conv in ((slice(0, half_rows), top), (slice(half_rows, rows), bottom)):
            value = vbuf[part, lanes].astype(jnp.float32)
            gate = gbuf[part, lanes].astype(jnp.float32)
            out_ref[part, lanes] = (gate * (conv + skip * value)).astype(jnp.bfloat16)
    for block in range(count):

        @pl.when(block != me)
        def _():
            back(block).wait_send()


def solution(mesh):
    count = mesh.shape["ctx"]
    lag_count = mesh.shape["lag"]

    def body(values, gate, bias, filter_taps):
        rows = values.shape[0]
        share = values.shape[1] // lag_count
        forward, inverse = tables(rows)
        any_spec = pl.BlockSpec(memory_space=pltpu.HBM)
        bf16, f32 = jnp.bfloat16, jnp.float32
        return pl.pallas_call(
            functools.partial(kernel, count),
            out_shape=pltpu.VMEM((rows, share), bf16),
            in_specs=[any_spec] * 6,
            out_specs=pl.BlockSpec(memory_space=pltpu.VMEM),
            scratch_shapes=[
                pltpu.VMEM((rows, share), bf16),
                pltpu.VMEM((rows, share), bf16),
                pltpu.VMEM((rows, share), bf16),
                pltpu.VMEM((1, share), f32),
                pltpu.VMEM((4 * rows, rows), bf16),
                pltpu.VMEM((rows, 2 * rows), bf16),
                pltpu.VMEM((count, rows, LANES), bf16),
                pltpu.VMEM((count, rows, LANES), bf16),
                pltpu.VMEM((count, 2 * rows, LANES), f32),
                pltpu.VMEM((count // 2, 2 * rows, LANES), f32),
                pltpu.VMEM((2 * rows, LANES), f32),
                pltpu.VMEM((count, 3, rows, LANES), f32),
                pltpu.VMEM((count, 2 * rows, LANES), bf16),
                pltpu.VMEM((count, rows // 2, LANES), bf16),
                pltpu.VMEM((count, rows // 2, LANES), bf16),
                pltpu.SemaphoreType.DMA((6,)),
                pltpu.SemaphoreType.DMA((count,)),
                pltpu.SemaphoreType.DMA((count,)),
                pltpu.SemaphoreType.DMA((count,)),
                pltpu.SemaphoreType.DMA((count,)),
            ],
            compiler_params=pltpu.CompilerParams(
                collective_id=0, has_side_effects=True, vmem_limit_bytes=60 * 2**20
            ),
            name="gated_conv",
        )(
            values,
            filter_taps,
            gate,
            bias.reshape(1, -1),
            jnp.asarray(np.concatenate(forward, axis=0)),
            jnp.asarray(inverse[0]),
        )

    return jax.shard_map(
        body,
        mesh=mesh,
        in_specs=(P("ctx", "chan"), P("ctx", ("chan", "lag")), P("chan"), P("ctx", "chan")),
        out_specs=P("ctx", ("chan", "lag")),
        check_vma=False,
    )
```

```python
import functools
import math

import jax
import jax.numpy as jnp
import numpy as np
from jax import lax
from jax.experimental import pallas as pl
from jax.experimental.pallas import tpu as pltpu
from jax.sharding import PartitionSpec as P

MESH = pl.DeviceIdType.MESH
LANES = 128
HALF = 64


def halves(table):
    upper = table.astype(jnp.bfloat16)
    lower = (table - upper.astype(np.float64)).astype(jnp.bfloat16)
    return upper, lower


def tables(rows):
    length = 2 * rows
    order = np.arange(rows)
    freq = np.where(order < rows // 2, 2 * order, 2 * (order - rows // 2) + 1)
    token = np.arange(rows)
    angle = 2.0 * math.pi * ((freq[:, None] * token[None, :]) % length) / length
    alternate = np.where(token % 2 == 0, 1.0, -1.0)
    real, imag = np.cos(angle), -np.sin(angle)
    imag[0] = alternate
    weight = np.where(order == 0, 1.0, 2.0) / length
    back_real = (real * weight[:, None]).T
    back_imag = (imag * weight[:, None]).T
    back_imag[:, 0] = -alternate / length
    forward = np.concatenate([real, imag], axis=0)
    backward = np.concatenate([back_real, back_imag], axis=1)
    return halves(forward), halves(backward)


MASKS = (10, 14, 6, 11, 9, 8, 2, 15, 5, 13, 7, 12, 4, 3, 1)


def kernel(
    count,
    values_hbm,
    taps_hbm,
    gate_hbm,
    bias_hbm,
    fwd_hbm,
    inv_hbm,
    out_ref,
    vbuf,
    tbuf,
    gbuf,
    bbuf,
    fwd,
    inv,
    packed,
    blocks,
    spec,
    turned,
    last,
    partial,
    total,
    ret_send,
    ret_recv,
    load_sem,
    send_sem,
    recv_sem,
    back_send_sem,
    back_recv_sem,
):
    me = lax.axis_index("ctx")
    lag = lax.axis_index("lag")
    rows, share = vbuf.shape
    half_rows = rows // 2
    tiles = share // LANES
    middle = count // 2
    quarter = count // 4
    peers = [me ^ mask for mask in MASKS]

    barrier = pltpu.get_barrier_semaphore()
    for peer in peers:
        pl.semaphore_signal(barrier, inc=1, device_id={"ctx": peer}, device_id_type=MESH)

    columns = pl.ds(pl.multiple_of(lag * share, share), share)
    loads = [
        pltpu.make_async_copy(src, dst, load_sem.at[i])
        for i, (src, dst) in enumerate(
            [
                (taps_hbm.at[:, columns], tbuf),
                (values_hbm.at[:, columns], vbuf),
                (fwd_hbm, fwd),
                (inv_hbm, inv),
                (bias_hbm.at[:, columns], bbuf),
                (gate_hbm, gbuf),
            ]
        )
    ]
    for load in loads[:2]:
        load.start()
    for load in loads[2:]:
        load.start()
    loads[0].wait()
    loads[1].wait()

    lower = lax.broadcasted_iota(jnp.int32, (rows, LANES), 1) < HALF
    for tile in range(tiles):
        lanes = slice(tile * LANES, (tile + 1) * LANES)
        value = vbuf[:, lanes].astype(jnp.float32)
        tap = pltpu.roll(tbuf[:, lanes].astype(jnp.float32), HALF, 1)
        packed[2 * tile] = jnp.where(lower, value, tap).astype(jnp.bfloat16)
        packed[2 * tile + 1] = jnp.where(lower, tap, value).astype(jnp.bfloat16)
    blocks[me] = packed[me]
    for load in loads[2:]:
        load.wait()

    pl.semaphore_wait(barrier, count - 1)

    def send(peer):
        return pltpu.make_async_remote_copy(
            src_ref=packed.at[peer],
            dst_ref=blocks.at[me],
            send_sem=send_sem.at[peer],
            recv_sem=recv_sem.at[me],
            device_id={"ctx": peer},
            device_id_type=MESH,
        )

    for peer in peers:
        send(peer).start()

    def arrival(buffer, sem, source):
        @pl.when(me != source)
        def _():
            pltpu.make_async_remote_copy(
                src_ref=buffer.at[source],
                dst_ref=buffer.at[source],
                send_sem=send_sem.at[0],
                recv_sem=sem.at[source],
                device_id={"ctx": source},
                device_id_type=MESH,
            ).wait_recv()

    def row_blocks(row):
        return range(row * quarter, (row + 1) * quarter)

    def transform(row):
        members = row_blocks(row)
        for block in members:
            arrival(blocks, recv_sem, block)
        for block in members[::2]:
            pair = jnp.concatenate([blocks[block], blocks[block + 1]], axis=1)
            both = jnp.dot(fwd[...], pair, preferred_element_type=jnp.float32)
            spectra = both[: 2 * rows] + both[2 * rows :]
            for k in range(2):
                spectrum = spectra[:, k * LANES : (k + 1) * LANES]
                spec[block + k] = spectrum
                if block < middle:
                    turned[block + k] = pltpu.roll(spectrum, HALF, 1)

    sub = lax.broadcasted_iota(jnp.int32, (8, LANES), 0)

    begun, closed = set(), []

    def products(pairs, close):
        closing = [n for row in close for n in range(row * quarter, (row + 1) * quarter)]
        touched = sorted({a + b for a, b in pairs} | set(closing))
        loaded = [n for n in touched if n in begun]
        first_close = not closed
        lefts = sorted({a for a, _ in pairs})
        rights = sorted({b for _, b in pairs})

        def group(step, carry):
            sign = jnp.where(step < rows // 32, 1.0, -1.0)
            parts = []
            for part in range(2):
                start = pl.multiple_of(step * 16 + part * 8, 8)
                real_rows = pl.ds(start, 8)
                imag_rows = pl.ds(pl.multiple_of(rows + start, 8), 8)
                mask = jnp.where(sub + start > 0, 1.0, 0.0)

                def triple(ref, block):
                    real, imag = ref[block, real_rows], ref[block, imag_rows]
                    return real, imag, real + imag

                acc = {}
                for n in loaded:
                    acc[n] = tuple(partial[n, k, real_rows] for k in range(3))
                right = {b: triple(spec, b) for b in rights}
                for a in lefts:
                    left = triple(turned, a)
                    for b in rights:
                        if (a, b) not in pairs:
                            continue
                        other = right[b] if a != b else tuple(0.5 * r for r in right[b])
                        terms = tuple(x * y for x, y in zip(left, other))
                        old = acc.get(a + b)
                        acc[a + b] = (
                            terms if old is None else tuple(x + y for x, y in zip(old, terms))
                        )
                for n in touched:
                    if n not in closing:
                        for k in range(3):
                            partial[n, k, real_rows] = acc[n][k]
                if not closing:
                    continue
                mixed = []
                before = None if first_close else (last[real_rows], last[imag_rows])
                for n in closing:
                    first, second, third = acc[n]
                    now = (first - mask * second, mask * (third - first) - second)
                    if before is None:
                        mixed.append(now)
                    else:
                        mixed.append((now[0] + sign * before[0], now[1] + sign * before[1]))
                    before = now
                if closing[-1] < count - 1:
                    last[real_rows] = before[0]
                    last[imag_rows] = before[1]
                parts.append(mixed)
            if not closing:
                return carry
            start = pl.multiple_of(step * 16, 16)
            for n, upper, under in zip(closing, *parts):
                total[n, pl.ds(start, 16)] = jnp.concatenate(
                    [upper[0], under[0]], axis=0
                ).astype(jnp.bfloat16)
                total[n, pl.ds(pl.multiple_of(rows + start, 16), 16)] = jnp.concatenate(
                    [upper[1], under[1]], axis=0
                ).astype(jnp.bfloat16)
            return carry

        lax.fori_loop(0, rows // 16, group, 0, unroll=True)
        begun.update(touched)
        closed.extend(closing)

    lower_half = lax.broadcasted_iota(jnp.int32, (half_rows, LANES), 1) < HALF

    def restore(first, second):
        pair = jnp.concatenate([total[first], total[second]], axis=1)
        both = jnp.dot(inv[...], pair, preferred_element_type=jnp.float32)
        results = both
        for k, block in enumerate((first, second)):
            result = results[:, k * LANES : (k + 1) * LANES]
            top, bottom = result[:half_rows], result[half_rows:]
            kept = jnp.where(lower_half, top, bottom)
            moved = pltpu.roll(jnp.where(lower_half, bottom, top), HALF, 1)
            ret_send[block] = (kept + moved).astype(jnp.bfloat16)

    def back(block):
        return pltpu.make_async_remote_copy(
            src_ref=ret_send.at[block],
            dst_ref=ret_recv.at[me],
            send_sem=back_send_sem.at[block],
            recv_sem=back_recv_sem.at[me],
            device_id={"ctx": block},
            device_id_type=MESH,
        )

    def finish(*groups):
        for members in groups:
            for first, second in zip(members[::2], members[1::2]):
                restore(first, second)
            for block in members:

                @pl.when(block != me)
                def _():
                    back(block).start()

    def pairs_of(left, right):
        return [
            (a, b)
            for a in row_blocks(left)
            for b in row_blocks(right)
            if a <= b and a + b < count
        ]

    transform(3)
    transform(2)
    transform(0)
    products(pairs_of(0, 0), [0])
    finish([0, 1])
    products(pairs_of(0, 2) + pairs_of(0, 3), [])
    transform(1)
    products(pairs_of(0, 1) + pairs_of(1, 1), [1])
    finish([4, 5, 3, 2])
    products(pairs_of(1, 2), [2])
    finish([8, 9, 7, 6])
    products([], [3])
    finish([12, 13, 11, 10], [15, 14])
    ret_recv[me] = ret_send[me]
    for peer in peers:
        send(peer).wait_send()

    for tile in range(tiles):
        lanes = slice(tile * LANES, (tile + 1) * LANES)
        arrival(ret_recv, back_recv_sem, 2 * tile)
        arrival(ret_recv, back_recv_sem, 2 * tile + 1)
        even = ret_recv[2 * tile].astype(jnp.float32)
        odd = ret_recv[2 * tile + 1].astype(jnp.float32)
        top = jnp.where(lower_half, even, pltpu.roll(odd, HALF, 1))
        bottom = jnp.where(lower_half, pltpu.roll(even, HALF, 1), odd)
        skip = bbuf[:, lanes]
        for part, conv in ((slice(0, half_rows), top), (slice(half_rows, rows), bottom)):
            value = vbuf[part, lanes].astype(jnp.float32)
            gate = gbuf[part, lanes].astype(jnp.float32)
            out_ref[part, lanes] = (gate * (conv + skip * value)).astype(jnp.bfloat16)
    for block in range(count):

        @pl.when(block != me)
        def _():
            back(block).wait_send()


def solution(mesh):
    count = mesh.shape["ctx"]
    lag_count = mesh.shape["lag"]

    def body(values, gate, bias, filter_taps):
        rows = values.shape[0]
        share = values.shape[1] // lag_count
        forward, inverse = tables(rows)
        any_spec = pl.BlockSpec(memory_space=pltpu.HBM)
        bf16, f32 = jnp.bfloat16, jnp.float32
        return pl.pallas_call(
            functools.partial(kernel, count),
            out_shape=pltpu.VMEM((rows, share), bf16),
            in_specs=[any_spec] * 6,
            out_specs=pl.BlockSpec(memory_space=pltpu.VMEM),
            scratch_shapes=[
                pltpu.VMEM((rows, share), bf16),
                pltpu.VMEM((rows, share), bf16),
                pltpu.VMEM((rows, share), bf16),
                pltpu.VMEM((1, share), f32),
                pltpu.VMEM((4 * rows, rows), bf16),
                pltpu.VMEM((rows, 2 * rows), bf16),
                pltpu.VMEM((count, rows, LANES), bf16),
                pltpu.VMEM((count, rows, LANES), bf16),
                pltpu.VMEM((count, 2 * rows, LANES), f32),
                pltpu.VMEM((count // 2, 2 * rows, LANES), f32),
                pltpu.VMEM((2 * rows, LANES), f32),
                pltpu.VMEM((count, 3, rows, LANES), f32),
                pltpu.VMEM((count, 2 * rows, LANES), bf16),
                pltpu.VMEM((count, rows // 2, LANES), bf16),
                pltpu.VMEM((count, rows // 2, LANES), bf16),
                pltpu.SemaphoreType.DMA((6,)),
                pltpu.SemaphoreType.DMA((count,)),
                pltpu.SemaphoreType.DMA((count,)),
                pltpu.SemaphoreType.DMA((count,)),
                pltpu.SemaphoreType.DMA((count,)),
            ],
            compiler_params=pltpu.CompilerParams(
                collective_id=0, has_side_effects=True, vmem_limit_bytes=60 * 2**20
            ),
            name="gated_conv",
        )(
            values,
            filter_taps,
            gate,
            bias.reshape(1, -1),
            jnp.asarray(np.concatenate(forward, axis=0)),
            jnp.asarray(inverse[0]),
        )

    return jax.shard_map(
        body,
        mesh=mesh,
        in_specs=(P("ctx", "chan"), P("ctx", ("chan", "lag")), P("chan"), P("ctx", "chan")),
        out_specs=P("ctx", ("chan", "lag")),
        check_vma=False,
    )
```
